32 devices in a mesh: dp: 8 (over z, y), tensor: 4 (over x, core).
Axes of the slice: x: 2, y: 2, z: 4, core: 2. Of those that a mesh axis runs over, the one named last changes fastest.
Arguments:
- tokens: bfloat16 [2, 8192, 768], P(None, ('dp', 'tensor')), may hold values from -6 to 6
- doc_ids: int32 [2, 8192], P(None, 'dp'), may hold values from 0 to 15, as said below
- live_mask: int32 [2, 8192], P(None, 'dp'), may hold values from 0 to 1, as said below
- attn_gain: float32 [768], replicated, may hold values from 0.25 to 1.75
- qkv_weight: bfloat16 [3, 768, 768], P(None, 'dp', 'tensor'), may hold values from -0.21875 to 0.21875
- attn_inner_gain: float32 [768], P('tensor'), may hold values from 0.25 to 1.75
- proj_weight: bfloat16 [768, 768], P('tensor', 'dp'), may hold values from -0.21875 to 0.21875
- ffn_gain: float32 [768], replicated, may hold values from 0.25 to 1.75
- up_weight: bfloat16 [768, 3072], P('dp', 'tensor'), may hold values from -0.21875 to 0.21875
- ffn_inner_gain: float32 [3072], P('tensor'), may hold values from 0.25 to 1.75
- down_weight: bfloat16 [3072, 768], P('tensor', 'dp'), may hold values from -0.109375 to 0.109375
- cotangent: bfloat16 [2, 8192, 768], P(None, ('dp', 'tensor')), may hold values from -6 to 6
Outputs:
- layer_out: float32 [2, 8192, 768], P(None, ('dp', 'tensor'))
- grad_tokens: float32 [2, 8192, 768], P(None, ('dp', 'tensor'))
- grad_attn_gain: float32 [768], replicated
- grad_qkv: float32 [3, 768, 768], P(None, 'dp', 'tensor')
- grad_attn_inner: float32 [768], P('tensor')
- grad_proj: float32 [768, 768], P('tensor', 'dp')
- grad_ffn_gain: float32 [768], replicated
- grad_up: float32 [768, 3072], P('dp', 'tensor')
- grad_ffn_inner: float32 [3072], P('tensor')
- grad_down: float32 [3072, 768], P('tensor', 'dp')
The draws below stay inside these ranges and needn't reach their ends.
Inputs may be any that keep to these rules, and one draw needn't show every extreme that they name: `doc_ids`: within each pack document numbers start at 0 and never fall; every document has 64 to 1024 tokens; in every draw some pack begins with a document of exactly 1024 tokens and some pack is made of documents of exactly 64 tokens; tokens after a pack's last whole document carry one more number. `live_mask`: 1 on the tokens of every whole document, 0 on the tokens after a pack's last whole document.
All inputs are finite; a program needn't handle non-finite values.
Results may differ from the reference program's by a relative error of at most 0.013.
Values may be sent and summed in bfloat16 or wider, within the bound.
No kernel may reach another device: no remote copies, remote signals or barrier semaphores. Data moves between devices by JAX's collectives and lax.ppermute only.
A program may use at most 128 MiB of HBM per device.

```python
import jax
import jax.numpy as jnp
from jax import lax

D = 768
HEADS = 12
HD = 64
FF = 3072
PACK = 1024
MICRO = 2
SHORTEST = 64
LONGEST = 2048
TOKENS_MB = 8192
N_DP = 8


def pack_layout(key):
    base = jax.random.fold_in(key, 4711)
    pack_count = MICRO * (TOKENS_MB // PACK)
    candidates = PACK // SHORTEST + 1
    top_bits = (LONGEST // SHORTEST).bit_length() - 1
    longest_here = min(PACK, LONGEST)
    key_exp, key_extra, key_pick = jax.random.split(base, 3)
    exponent = jax.random.randint(key_exp, (pack_count, candidates), 0, top_bits + 1)
    unit_len = jnp.left_shift(jnp.full((pack_count, candidates), SHORTEST, jnp.int32), exponent)
    extra_len = jax.random.randint(key_extra, (pack_count, candidates), 0, 1 << 30) % unit_len
    lengths = jnp.minimum(unit_len + extra_len, longest_here)
    chosen = jax.random.randint(key_pick, (), 0, pack_count)
    pack_places = jnp.arange(pack_count)
    dense_pack = pack_places == (chosen + 1) % pack_count
    lengths = jnp.where(dense_pack[:, None], SHORTEST, lengths)
    first_len = jnp.where(pack_places == chosen, longest_here, lengths[:, 0])
    lengths = jnp.concatenate([first_len[:, None], lengths[:, 1:]], axis=1).astype(jnp.int32)
    doc_ends = jnp.cumsum(lengths, axis=1)
    places = jnp.arange(PACK, dtype=jnp.int32)
    numbers = jnp.sum((doc_ends[:, None, :] <= places[None, :, None]).astype(jnp.int32), axis=2)
    whole_docs = jnp.sum((doc_ends <= PACK).astype(jnp.int32), axis=1)
    last_end = jnp.max(jnp.where(doc_ends <= PACK, doc_ends, 0), axis=1)
    numbers = jnp.minimum(numbers, whole_docs[:, None]).astype(jnp.int32)
    live_rows = (places[None, :] < last_end[:, None]).astype(jnp.int32)
    return (numbers.reshape(MICRO, TOKENS_MB), live_rows.reshape(MICRO, TOKENS_MB))


def draw_doc_ids(key, part):
    return pack_layout(key)[0]


def draw_live_mask(key, part):
    return pack_layout(key)[1]


def level_of(key, dims, pieces, smallest, top_value):
    loudness, own = 1.0, jax.random.fold_in(key, 6)
    for position, blocks in pieces:
        heights = jnp.exp(jax.random.uniform(jax.random.fold_in(own, position), (blocks,), jnp.float32, smallest / len(pieces), top_value / len(pieces)))
        loudness = loudness * jnp.repeat(heights, dims[position] // blocks).reshape([-1 if axis == position else 1 for axis in range(len(dims))])
    return loudness


def normal_values(own_key, shape, scale, bound, shards=(), held_as=jnp.bfloat16):
    drawn = jax.random.normal(own_key, shape, jnp.float32) * scale
    if len(shards) > 0:
        drawn = level_of(own_key, shape, shards, -0.22, 0.18) * drawn
    return jnp.clip(drawn, min=-bound, max=bound).astype(held_as)


def setup_inputs(seed: int = 0) -> dict:
    key_of = jax.random.split(jax.random.key(seed), 13)
    tokens = normal_values(key_of[0], (MICRO, TOKENS_MB, D), 1.0, 6.0, ((1, 32),))
    doc_ids = draw_doc_ids(jax.random.fold_in(key_of[12], 71), 0)
    live_mask = draw_live_mask(jax.random.fold_in(key_of[12], 71), 0)
    attn_gain = jnp.clip(1.0 + 0.15 * jax.random.normal(key_of[3], (D,), jnp.float32), 0.25, 1.75)
    qkv_weight = normal_values(key_of[4], (3, D, D), D ** -0.5, 0.21875, ((1, 8), (2, 4)))
    attn_inner_gain = jnp.clip(1.0 + 0.15 * jax.random.normal(key_of[5], (D,), jnp.float32), 0.25, 1.75)
    proj_weight = normal_values(key_of[6], (D, D), D ** -0.5, 0.21875, ((0, 4), (1, 8)))
    ffn_gain = jnp.clip(1.0 + 0.15 * jax.random.normal(key_of[7], (D,), jnp.float32), 0.25, 1.75)
    up_weight = normal_values(key_of[8], (D, FF), D ** -0.5, 0.21875, ((0, 8), (1, 4)))
    ffn_inner_gain = jnp.clip(1.0 + 0.15 * jax.random.normal(key_of[9], (FF,), jnp.float32), 0.25, 1.75)
    down_weight = normal_values(key_of[10], (FF, D), FF ** -0.5, 0.109375, ((0, 4), (1, 8)))
    cotangent = normal_values(key_of[11], (MICRO, TOKENS_MB, D), 1.0, 6.0, ((1, 32),))
    return {"tokens": tokens, "doc_ids": doc_ids, "live_mask": live_mask, "attn_gain": attn_gain, "qkv_weight": qkv_weight, "attn_inner_gain": attn_inner_gain, "proj_weight": proj_weight, "ffn_gain": ffn_gain, "up_weight": up_weight, "ffn_inner_gain": ffn_inner_gain, "down_weight": down_weight, "cotangent": cotangent}


@jax.custom_vjp
def low(v):
    return lax.optimization_barrier(v.astype(jnp.bfloat16)).astype(jnp.float32)

@jax.custom_vjp
def low_back(v):
    return v

def low_keep(v):
    return (low(v), None)

def low_pass(kept, grad):
    return (grad,)

def back_keep(v):
    return (v, None)

def back_low(kept, grad):
    return (low(grad),)
low.defvjp(low_keep, low_pass)
low_back.defvjp(back_keep, back_low)
eps_norm = 1e-05
highest = lax.Precision.HIGHEST

def layer_norm(values, gain_vec):
    row_mean = lax.optimization_barrier(jnp.mean(values, axis=-1, keepdims=True))
    row_var = lax.optimization_barrier(jnp.mean(values * values, axis=-1, keepdims=True)) - row_mean * row_mean
    return (values - row_mean) * lax.rsqrt(row_var + eps_norm) * gain_vec

def block_attention(query_rows, key_all, value_all, doc_query, doc_all, first_row):
    raw_scores = jnp.einsum('qhd,khd->hqk', query_rows, key_all, precision=highest) * HD ** (-0.5)
    raw_scores = low_back(raw_scores)
    place_query = first_row + jnp.arange(query_rows.shape[0], dtype=jnp.int32)
    place_key = jnp.arange(key_all.shape[0], dtype=jnp.int32)
    allowed = (doc_query[:, None] == doc_all[None, :]) & (place_key[None, :] <= place_query[:, None])
    probs = low(jax.nn.softmax(jnp.where(allowed[None], raw_scores, -jnp.inf), axis=-1))
    return jnp.einsum('hqk,khd->qhd', probs, value_all, precision=highest)

def pack_layer(xin, doc_all, live_rows, attn_gain, qkv_weight, attn_inner_gain, proj_weight, ffn_gain, up_weight, ffn_inner_gain, down_weight):
    row_count = xin.shape[0]
    normed_a = low(layer_norm(xin, attn_gain))
    projected = low(low_back(jnp.einsum('td,sde->ste', normed_a, qkv_weight, precision=highest)))
    heads_all = projected.reshape(3, row_count, HEADS, HD)
    block_rows = min(512, row_count)
    block_count = row_count // block_rows
    key_all = heads_all[1]
    value_all = heads_all[2]

    def one_block(block_item):
        return jax.checkpoint(block_attention)(block_item[0], key_all, value_all, block_item[1], doc_all, block_item[2])
    starts = jnp.arange(block_count, dtype=jnp.int32) * block_rows
    attended = lax.map(one_block, (heads_all[0].reshape(block_count, block_rows, HEADS, HD), doc_all.reshape(block_count, block_rows), starts))
    attended = low_back(attended.reshape(row_count, D)) * live_rows[:, None]
    inner_a = low(layer_norm(attended, attn_inner_gain))
    branch_a = low_back(jnp.dot(inner_a, proj_weight, precision=highest))
    mid = xin + branch_a
    normed_f = low(layer_norm(mid, ffn_gain))
    hidden = low_back(jnp.dot(normed_f, up_weight, precision=highest))
    inner_f = low(layer_norm(jax.nn.gelu(hidden, approximate=False), ffn_inner_gain))
    branch_f = low_back(jnp.dot(inner_f, down_weight, precision=highest))
    return mid + branch_f

def reference(tokens, doc_ids, live_mask, attn_gain, qkv_weight, attn_inner_gain, proj_weight, ffn_gain, up_weight, ffn_inner_gain, down_weight, cotangent):
    pack_count = MICRO * N_DP
    packed_x = tokens.astype(jnp.float32).reshape(pack_count, PACK, D)
    packed_doc = doc_ids.reshape(pack_count, PACK).astype(jnp.int32)
    packed_live = live_mask.reshape(pack_count, PACK).astype(jnp.float32)
    params = (attn_gain.astype(jnp.float32), qkv_weight.astype(jnp.float32), attn_inner_gain.astype(jnp.float32), proj_weight.astype(jnp.float32), ffn_gain.astype(jnp.float32), up_weight.astype(jnp.float32), ffn_inner_gain.astype(jnp.float32), down_weight.astype(jnp.float32))

    def forward(all_x, all_params):

        def pack_step(carry, pack_item):
            return (carry, pack_layer(pack_item[0], pack_item[1], pack_item[2], *all_params))
        unused, outputs = lax.scan(pack_step, jnp.float32(0.0), (all_x, packed_doc, packed_live))
        return outputs
    outputs, pull_back = jax.vjp(forward, packed_x, params)
    grad_x, grad_params = pull_back(cotangent.astype(jnp.float32).reshape(pack_count, PACK, D))
    shape_out = (MICRO, TOKENS_MB, D)
    return (outputs.reshape(shape_out), grad_x.reshape(shape_out), grad_params[0], grad_params[1], grad_params[2], grad_params[3], grad_params[4], grad_params[5], grad_params[6], grad_params[7])
```

```python
import functools

import jax
import jax.numpy as jnp
from jax import lax
from jax.experimental import pallas as pl
from jax.experimental.pallas import tpu as pltpu
from jax.sharding import PartitionSpec as P

D = 768
HD = 64
FF = 3072
EPS = 1e-05
BLK = 256
SCALE = HD ** (-0.5)
NEG = -1e30
BF = jnp.bfloat16
F4 = jnp.float32
SQRT_HALF = 0.7071067811865476
INV_SQRT_2PI = 0.3989422804014327


def dot_nn(a, b):
    return lax.dot_general(a, b, (((1,), (0,)), ((), ())), preferred_element_type=F4)


def dot_nt(a, b):
    return lax.dot_general(a, b, (((1,), (1,)), ((), ())), preferred_element_type=F4)


def dot_tn(a, b):
    return lax.dot_general(a, b, (((0,), (0,)), ((), ())), preferred_element_type=F4)


def over_tensor(value, bit):
    size = lax.axis_size("tensor")
    return lax.ppermute(value, "tensor", [(i, i ^ bit) for i in range(size)])


def over_dp_bit(value, bit):
    size = lax.axis_size("dp")
    return lax.ppermute(value, "dp", [(i, i ^ bit) for i in range(size)])


def over_z(value, step):
    size = lax.axis_size("dp")
    return lax.ppermute(value, "dp", [(i, (i + 2 * step) % size) for i in range(size)])


def gather_ring(shard, z_place, y_place):
    half = shard.shape[0] // 2
    others = [over_z(shard, k) for k in (1, 2, 3)]
    upper = jnp.stack([shard[:half]] + [o[:half] for o in others])
    lower = jnp.stack([shard[half:]] + [o[half:] for o in others])
    upper_x = over_tensor(upper, 2)
    lower_y = over_dp_bit(lower, 1)
    upper_y = over_dp_bit(jnp.stack([upper, upper_x]), 1)
    lower_x = over_tensor(jnp.stack([lower, lower_y]), 2)
    rel = jnp.stack(
        [
            jnp.stack(
                [jnp.stack([upper, upper_y[0]], 1), jnp.stack([lower, lower_y], 1)], 2
            ),
            jnp.stack(
                [jnp.stack([upper_x, upper_y[1]], 1), jnp.stack([lower_x[0], lower_x[1]], 1)], 2
            ),
        ]
    )
    rel = jnp.where(y_place == 0, rel, rel[:, :, ::-1])
    back = rel[:, ::-1]
    twice = jnp.concatenate([back, back], axis=1)
    full = lax.dynamic_slice_in_dim(twice, 3 - z_place, 4, axis=1)
    return full.reshape(2, D, D)


def gather_any(shard):
    own = lax.all_gather(shard, "dp", axis=0, tiled=True)
    return jnp.stack([own, over_tensor(own, 2)])


def scatter_ring(grad, z_place, y_place):
    cols = grad.shape[-1]
    parts = grad.reshape(2, 4, 2, 2, D // 16, cols)
    upper = parts[:, :, :, 0]
    lower = parts[:, :, :, 1]
    send_u = lax.dynamic_index_in_dim(upper, 1 - y_place, 2, keepdims=False).astype(BF)
    keep_u = lax.dynamic_index_in_dim(upper, y_place, 2, keepdims=False)
    recv_u = over_dp_bit(send_u, 1).astype(F4)
    recv_l = over_tensor(lower[1].astype(BF), 2).astype(F4)
    mid_u = keep_u + recv_u
    mid_l = lower[0] + recv_l
    recv_u2 = over_tensor(mid_u[1].astype(BF), 2).astype(F4)
    send_l = lax.dynamic_index_in_dim(mid_l, 1 - y_place, 1, keepdims=False).astype(BF)
    keep_l = lax.dynamic_index_in_dim(mid_l, y_place, 1, keepdims=False)
    recv_l2 = over_dp_bit(send_l, 1).astype(F4)
    rows = jnp.concatenate([mid_u[0] + recv_u2, keep_l + recv_l2], axis=1)
    total = lax.dynamic_index_in_dim(rows, z_place, 0, keepdims=False)
    for step in (1, 2, 3):
        part = lax.dynamic_index_in_dim(rows, (z_place + step) % 4, 0, keepdims=False)
        total = total + over_z(part.astype(BF), step).astype(F4)
    return total


def scatter_any(grad):
    total = grad[0] + over_tensor(grad[1].astype(BF), 2).astype(F4)
    return lax.psum_scatter(total, "dp", scatter_dimension=0, tiled=True)


def sum_everywhere(vector):
    vector = vector + over_tensor(vector, 1)
    vector = vector + over_tensor(vector, 2)
    bit = 1
    while bit < lax.axis_size("dp"):
        vector = vector + over_dp_bit(vector, bit)
        bit *= 2
    return vector


def attn_fwd_kernel(normed_ref, w_ref, doc_col_ref, doc_row_ref, proj_ref, att_ref, lse_ref, bias_ref):
    rows = normed_ref.shape[0]

    @pl.when(pl.program_id(0) == 0)
    def _():
        for i in range(rows // BLK):
            same = doc_col_ref[pl.ds(i * BLK, BLK), :] == doc_row_ref[:, : (i + 1) * BLK]
            row_id = i * BLK + lax.broadcasted_iota(jnp.int32, same.shape, 0)
            col_id = lax.broadcasted_iota(jnp.int32, same.shape, 1)
            bias_ref[pl.ds(i * BLK, BLK), : (i + 1) * BLK] = jnp.where(
                same & (col_id <= row_id), 0.0, NEG
            )

    proj_ref[0] = dot_nn(normed_ref[...], w_ref[0, :, : 9 * HD]).astype(BF)
    for h in range(3):
        keys = proj_ref[0, :, (3 + h) * HD : (4 + h) * HD]
        values = proj_ref[0, :, (6 + h) * HD : (7 + h) * HD]
        for i in range(rows // BLK):
            span = (i + 1) * BLK
            here = pl.ds(i * BLK, BLK)
            query = proj_ref[0, here, h * HD : (h + 1) * HD] * BF(SCALE)
            scores = dot_nt(query, keys[:span]) + bias_ref[here, :span]
            peak = jnp.max(scores, axis=-1, keepdims=True)
            terms = jnp.exp(scores - peak)
            total = jnp.sum(terms, axis=-1, keepdims=True)
            mixed = dot_nn(terms.astype(BF), values[:span]) / total
            att_ref[0, here, h * HD : (h + 1) * HD] = mixed
            lse_ref[0, here, h : h + 1] = peak + jnp.log(total)


def attn_forward(normed, weights, doc_all):
    rows = normed.shape[0]
    return pl.pallas_call(
        attn_fwd_kernel,
        grid=(2,),
        in_specs=[
            pl.BlockSpec((rows, D), lambda g: (0, 0)),
            pl.BlockSpec((1, D, D), lambda g: (g, 0, 0)),
            pl.BlockSpec((rows, 1), lambda g: (0, 0)),
            pl.BlockSpec((1, rows), lambda g: (0, 0)),
        ],
        out_specs=[
            pl.BlockSpec((1, rows, 9 * HD), lambda g: (g, 0, 0)),
            pl.BlockSpec((1, rows, 3 * HD), lambda g: (g, 0, 0)),
            pl.BlockSpec((1, rows, 128), lambda g: (g, 0, 0)),
        ],
        out_shape=[
            jax.ShapeDtypeStruct((2, rows, 9 * HD), BF),
            jax.ShapeDtypeStruct((2, rows, 3 * HD), F4),
            jax.ShapeDtypeStruct((2, rows, 128), F4),
        ],
        scratch_shapes=[pltpu.VMEM((rows, rows), F4)],
        cost_estimate=pl.CostEstimate(
            flops=2 * rows * D * 18 * HD + 4 * 6 * rows * rows * HD,
            transcendentals=6 * rows * rows // 2,
            bytes_accessed=8 * rows * D,
        ),
        compiler_params=pltpu.CompilerParams(vmem_limit_bytes=50 * 1024 * 1024),
        name="attn_fwd",
    )(normed, weights, doc_all.reshape(rows, 1), doc_all.reshape(1, rows))


def attn_bwd_kernel(
    normed_ref, w_ref, proj_ref, lse_ref, gatt_ref, doc_col_ref, doc_row_ref,
    gw_ref, dn_ref, bias_ref, gp_ref, gk_ref, gv_ref,
):
    rows = normed_ref.shape[0]

    @pl.when(pl.program_id(0) == 0)
    def _():
        for i in range(rows // BLK):
            span = (i + 1) * BLK
            same = doc_col_ref[:span, :] == doc_row_ref[:, i * BLK : span]
            key_id = lax.broadcasted_iota(jnp.int32, same.shape, 0)
            query_id = i * BLK + lax.broadcasted_iota(jnp.int32, same.shape, 1)
            bias_ref[:span, i * BLK : span] = jnp.where(same & (key_id <= query_id), 0.0, NEG)

    for h in range(3):
        keys = proj_ref[0, :, (3 + h) * HD : (4 + h) * HD]
        values = proj_ref[0, :, (6 + h) * HD : (7 + h) * HD]
        for i in reversed(range(rows // BLK)):
            span = (i + 1) * BLK
            here = pl.ds(i * BLK, BLK)
            query = proj_ref[0, here, h * HD : (h + 1) * HD] * BF(SCALE)
            grad_rows = gatt_ref[0, here, h * HD : (h + 1) * HD]
            scores = dot_nt(keys[:span], query) + bias_ref[:span, here]
            probs = jnp.exp(scores - lse_ref[0, h : h + 1, here])
            grad_probs = dot_nt(values[:span], grad_rows)
            inner = jnp.sum(probs * grad_probs, axis=0, keepdims=True)
            grad_scores = (probs * (grad_probs - inner)).astype(BF)
            add_v = dot_nn(probs.astype(BF), grad_rows)
            add_k = dot_nn(grad_scores, query)
            if span == rows:
                gv_ref[...] = add_v
                gk_ref[...] = add_k
            else:
                gv_ref[:span] += add_v
                gk_ref[:span] += add_k
            gp_ref[here, h * HD : (h + 1) * HD] = (
                dot_tn(grad_scores, keys[:span]) * SCALE
            ).astype(BF)
        gp_ref[:, (3 + h) * HD : (4 + h) * HD] = gk_ref[...].astype(BF)
        gp_ref[:, (6 + h) * HD : (7 + h) * HD] = gv_ref[...].astype(BF)
    gw_ref[0] = dot_tn(normed_ref[...], gp_ref[...])
    back = dot_nt(gp_ref[...], w_ref[0, :, : 9 * HD])

    @pl.when(pl.program_id(0) == 0)
    def _():
        dn_ref[...] = back

    @pl.when(pl.program_id(0) == 1)
    def _():
        dn_ref[...] += back


def attn_backward(normed, weights, projected, lse, grad_att, doc_all):
    rows = normed.shape[0]
    return pl.pallas_call(
        attn_bwd_kernel,
        grid=(2,),
        in_specs=[
            pl.BlockSpec((rows, D), lambda g: (0, 0)),
            pl.BlockSpec((1, D, D), lambda g: (g, 0, 0)),
            pl.BlockSpec((1, rows, 9 * HD), lambda g: (g, 0, 0)),
            pl.BlockSpec((1, 8, rows), lambda g: (g, 0, 0)),
            pl.BlockSpec((1, rows, 3 * HD), lambda g: (g, 0, 0)),
            pl.BlockSpec((rows, 1), lambda g: (0, 0)),
            pl.BlockSpec((1, rows), lambda g: (0, 0)),
        ],
        out_specs=[
            pl.BlockSpec((1, D, 9 * HD), lambda g: (g, 0, 0)),
            pl.BlockSpec((rows, D), lambda g: (0, 0)),
        ],
        out_shape=[
            jax.ShapeDtypeStruct((2, D, 9 * HD), F4),
            jax.ShapeDtypeStruct((rows, D), F4),
        ],
        scratch_shapes=[
            pltpu.VMEM((rows, rows), F4),
            pltpu.VMEM((rows, 9 * HD), BF),
            pltpu.VMEM((rows, HD), F4),
            pltpu.VMEM((rows, HD), F4),
        ],
        cost_estimate=pl.CostEstimate(
            flops=4 * rows * D * 18 * HD + 10 * 6 * rows * rows * HD,
            transcendentals=6 * rows * rows // 2,
            bytes_accessed=16 * rows * D,
        ),
        compiler_params=pltpu.CompilerParams(vmem_limit_bytes=50 * 1024 * 1024),
        name="attn_bwd",
    )(normed, weights, projected, lse, grad_att, doc_all.reshape(rows, 1), doc_all.reshape(1, rows))


def row_stats(values, width):
    mean = jnp.sum(values, axis=-1, keepdims=True) / width
    var = jnp.sum(values * values, axis=-1, keepdims=True) / width - mean * mean
    return mean, lax.rsqrt(var + EPS)


def middle_kernel(
    xin_ref, att_a_ref, att_b_ref, live_ref, cot_ref,
    proj_a_ref, proj_b_ref, up_a_ref, up_b_ref, down_a_ref, down_b_ref,
    gain_a_ref, gain_f_ref, gain_h_ref,
    out_ref, gmid_ref, gatt_a_ref, gatt_b_ref, inner_a_ref, inner_b_ref, normf_ref,
    hid_a_ref, hid_b_ref, gh_a_ref, gh_b_ref, branch_ref, gg_a_ref, gg_f_ref, gg_h_ref,
    act_ref, slope_ref, scaled_ref,
):
    first = pl.program_id(0) == 0
    live = live_ref[...]
    att = jnp.concatenate(
        [att_a_ref[0], att_a_ref[1], att_b_ref[0], att_b_ref[1]], axis=1
    ) * live
    mean_a, inv_a = row_stats(att, D)
    norm_a = (att - mean_a) * inv_a
    gain_a = gain_a_ref[...]
    inner = (norm_a * gain_a).astype(BF)
    inner_a_ref[...] = inner[:, : D // 2]
    inner_b_ref[...] = inner[:, D // 2 :]
    proj_t = jnp.concatenate(
        [proj_a_ref[0], proj_a_ref[1], proj_b_ref[0], proj_b_ref[1]], axis=1
    )
    mid = xin_ref[...].astype(F4) + dot_nt(inner, proj_t)
    mean_f, inv_f = row_stats(mid, D)
    norm_f = (mid - mean_f) * inv_f
    gain_f = gain_f_ref[...]
    normed_f = (norm_f * gain_f).astype(BF)
    normf_ref[...] = normed_f

    ups = [(up_a_ref, 0), (up_a_ref, 1), (up_b_ref, 0), (up_b_ref, 1)]
    downs = [(down_a_ref, 0), (down_a_ref, 1), (down_b_ref, 0), (down_b_ref, 1)]
    total = 0.0
    square = 0.0
    for j, (ref, k) in enumerate(ups):
        hidden = dot_nn(normed_f, ref[k])
        phi = 0.5 * (1.0 + lax.erf(hidden * SQRT_HALF))
        act = hidden * phi
        slope_ref[j] = phi + hidden * (INV_SQRT_2PI * jnp.exp(-0.5 * hidden * hidden))
        act_ref[j] = act
        total += jnp.sum(act, axis=-1, keepdims=True)
        square += jnp.sum(act * act, axis=-1, keepdims=True)
    mean_h = total / FF
    inv_h = lax.rsqrt(square / FF - mean_h * mean_h + EPS)
    cot = cot_ref[...]
    out = mid
    sum_s = 0.0
    sum_c = 0.0
    for j, (ref, k) in enumerate(downs):
        norm_h = (act_ref[j] - mean_h) * inv_h
        act_ref[j] = norm_h
        gain_h = gain_h_ref[:, j * D : (j + 1) * D]
        low = (norm_h * gain_h).astype(BF)
        if j < 2:
            hid_a_ref[:, j * D : (j + 1) * D] = low
        else:
            hid_b_ref[:, (j - 2) * D : (j - 1) * D] = low
        out = out + dot_nt(low, ref[k])
        grad_low = dot_nn(cot, ref[k])
        crossed = grad_low * norm_h
        gain_part = jnp.sum(crossed, axis=0, keepdims=True)

        @pl.when(first)
        def _(gain_part=gain_part, j=j):
            gg_h_ref[:, j * D : (j + 1) * D] = gain_part

        @pl.when(jnp.logical_not(first))
        def _(gain_part=gain_part, j=j):
            gg_h_ref[:, j * D : (j + 1) * D] += gain_part

        scaled = grad_low * gain_h
        scaled_ref[j] = scaled
        sum_s += jnp.sum(scaled, axis=-1, keepdims=True)
        sum_c += jnp.sum(crossed * gain_h, axis=-1, keepdims=True)
    out_ref[...] = out
    mean_s = sum_s / FF
    mean_c = sum_c / FF
    grad_n = 0.0
    for j, (ref, k) in enumerate(ups):
        grad_act = inv_h * (scaled_ref[j] - mean_s - act_ref[j] * mean_c)
        grad_hidden = (grad_act * slope_ref[j]).astype(BF)
        if j < 2:
            gh_a_ref[:, j * D : (j + 1) * D] = grad_hidden
        else:
            gh_b_ref[:, (j - 2) * D : (j - 1) * D] = grad_hidden
        grad_n = grad_n + dot_nt(grad_hidden, ref[k])
    gain_part_f = jnp.sum(grad_n * norm_f, axis=0, keepdims=True)
    scaled = grad_n * gain_f
    mean_s = jnp.sum(scaled, axis=-1, keepdims=True) / D
    mean_c = jnp.sum(scaled * norm_f, axis=-1, keepdims=True) / D
    grad_mid = cot.astype(F4) + inv_f * (scaled - mean_s - norm_f * mean_c)
    gmid_ref[...] = grad_mid
    branch = grad_mid.astype(BF)
    branch_ref[...] = branch
    grad_inner = dot_nn(branch, proj_t)
    gain_part_a = jnp.sum(grad_inner * norm_a, axis=0, keepdims=True)
    scaled = grad_inner * gain_a
    mean_s = jnp.sum(scaled, axis=-1, keepdims=True) / D
    mean_c = jnp.sum(scaled * norm_a, axis=-1, keepdims=True) / D
    grad_att = (inv_a * (scaled - mean_s - norm_a * mean_c) * live).astype(BF)
    quarter = 3 * HD
    gatt_a_ref[0] = grad_att[:, :quarter]
    gatt_a_ref[1] = grad_att[:, quarter : 2 * quarter]
    gatt_b_ref[0] = grad_att[:, 2 * quarter : 3 * quarter]
    gatt_b_ref[1] = grad_att[:, 3 * quarter :]

    @pl.when(first)
    def _():
        gg_f_ref[...] = gain_part_f
        gg_a_ref[...] = gain_part_a

    @pl.when(jnp.logical_not(first))
    def _():
        gg_f_ref[...] += gain_part_f
        gg_a_ref[...] += gain_part_a


def middle(xin, att_a, att_b, live, cot, proj_a, proj_b, up_a, up_b, down_a, down_b, gain_a, gain_f, gain_h):
    rows = xin.shape[0]
    steps = rows // BLK
    row = lambda g: (g, 0)
    deep = lambda g: (0, g, 0)
    fixed = lambda g: (0, 0)
    once = pl.Buffered(1)

    def rows_of(width):
        return pl.BlockSpec((BLK, width), row)

    quarter = 3 * HD
    heads = pl.BlockSpec((2, BLK, quarter), deep)

    def whole(width):
        return pl.BlockSpec((2, D, width), lambda g: (0, 0, 0), pipeline_mode=once)

    def vec(width):
        return pl.BlockSpec((1, width), fixed)

    return pl.pallas_call(
        middle_kernel,
        grid=(steps,),
        in_specs=[
            rows_of(D), heads, heads, rows_of(1), rows_of(D),
            whole(quarter), whole(quarter), whole(D), whole(D), whole(D), whole(D),
            vec(D), vec(D), vec(FF),
        ],
        out_specs=[
            rows_of(D), rows_of(D), heads, heads, rows_of(D // 2), rows_of(D // 2), rows_of(D),
            rows_of(FF // 2), rows_of(FF // 2), rows_of(FF // 2), rows_of(FF // 2), rows_of(D),
            vec(D), vec(D), vec(FF),
        ],
        out_shape=[
            jax.ShapeDtypeStruct((rows, D), F4),
            jax.ShapeDtypeStruct((rows, D), F4),
            jax.ShapeDtypeStruct((2, rows, quarter), BF),
            jax.ShapeDtypeStruct((2, rows, quarter), BF),
            jax.ShapeDtypeStruct((rows, D // 2), BF),
            jax.ShapeDtypeStruct((rows, D // 2), BF),
            jax.ShapeDtypeStruct((rows, D), BF),
            jax.ShapeDtypeStruct((rows, FF // 2), BF),
            jax.ShapeDtypeStruct((rows, FF // 2), BF),
            jax.ShapeDtypeStruct((rows, FF // 2), BF),
            jax.ShapeDtypeStruct((rows, FF // 2), BF),
            jax.ShapeDtypeStruct((rows, D), BF),
            jax.ShapeDtypeStruct((1, D), F4),
            jax.ShapeDtypeStruct((1, D), F4),
            jax.ShapeDtypeStruct((1, FF), F4),
        ],
        scratch_shapes=[pltpu.VMEM((4, BLK, D), F4)] * 3,
        cost_estimate=pl.CostEstimate(
            flops=4 * rows * D * (D + 2 * FF),
            transcendentals=2 * rows * FF,
            bytes_accessed=22 * 1024 * 1024,
        ),
        compiler_params=pltpu.CompilerParams(vmem_limit_bytes=60 * 1024 * 1024),
        name="middle",
    )(xin, att_a, att_b, live, cot, proj_a, proj_b, up_a, up_b, down_a, down_b, gain_a, gain_f, gain_h)


def weave(own, other, core):
    even = jnp.where(core == 0, own, other)
    odd = jnp.where(core == 0, other, own)
    stacked = jnp.stack([even, odd], axis=1)
    return stacked.reshape((-1,) + own.shape[2:])


def per_device(
    tokens,
    doc_ids,
    live_mask,
    attn_gain,
    qkv_weight,
    attn_inner_gain,
    proj_weight,
    ffn_gain,
    up_weight,
    ffn_inner_gain,
    down_weight,
    cotangent,
):
    ring = lax.axis_size("dp") == 8
    tensor_place = lax.axis_index("tensor")
    dp_place = lax.axis_index("dp")
    side = tensor_place // 2
    core = tensor_place % 2
    z_place, y_place = dp_place // 2, dp_place % 2
    chunk = tokens.shape[1]
    shard_rows = up_weight.shape[0]
    quarter = 3 * HD

    def gather(shard):
        return gather_ring(shard, z_place, y_place) if ring else gather_any(shard)

    def scatter(grad):
        return scatter_ring(grad, z_place, y_place) if ring else scatter_any(grad)

    def pick(pair, index):
        return lax.dynamic_index_in_dim(pair, index, 0, keepdims=False)

    def swap(pair):
        own = pick(pair, side)
        other = over_tensor(pick(pair, 1 - side), 2)
        return jnp.where(side == 0, jnp.stack([own, other]), jnp.stack([other, own]))

    def swap_back(both):
        own = pick(both, side)
        other = over_tensor(pick(both, 1 - side).astype(BF), 2).astype(F4)
        return jnp.where(side == 0, jnp.stack([own, other]), jnp.stack([other, own]))

    first_shard = jnp.concatenate(
        [qkv_weight[0], qkv_weight[1], qkv_weight[2], proj_weight.T], axis=1
    )
    first_own = gather(first_shard)
    up_own = gather(up_weight)
    down_own = gather(down_weight.T)
    proj_own = first_own[:, :, 9 * HD :]
    proj_other = over_tensor(proj_own, 1)
    up_other = over_tensor(up_own, 1)
    down_other = over_tensor(down_own, 1)
    gains = jnp.concatenate([attn_inner_gain, ffn_inner_gain]).reshape(1, -1)
    gain_all = jnp.stack(
        [gains, over_tensor(gains, 2), over_tensor(gains, 1), over_tensor(gains, 3)]
    )
    gain_inner = gain_all[:, 0, :quarter].reshape(1, D)
    gain_hidden = gain_all[:, 0, quarter:].reshape(1, FF)

    x_rows = swap(tokens)
    cot_rows = swap(cotangent)
    doc_all = pick(doc_ids, side)
    live_all = pick(live_mask, side).astype(F4).reshape(2, 2, chunk)
    live = lax.dynamic_index_in_dim(live_all, core, 1, keepdims=False).reshape(2 * chunk, 1)
    xin = x_rows.reshape(2 * chunk, D).astype(F4)
    mean_t, inv_t = row_stats(xin, D)
    norm_t = (xin - mean_t) * inv_t
    normed_own = (norm_t * attn_gain).astype(BF)
    normed_other = over_tensor(normed_own, 1)
    normed = weave(normed_own.reshape(2, chunk, D), normed_other.reshape(2, chunk, D), core)

    projected, attended, lse = attn_forward(normed, first_own, doc_all)
    lse_rows = jnp.pad(jnp.swapaxes(lse[:, :, :3], 1, 2), ((0, 0), (0, 5), (0, 0)))
    att_blocks = attended.reshape(2, 2, 2, chunk, quarter)
    att_mine = lax.dynamic_index_in_dim(att_blocks, core, 2, keepdims=False)
    att_send = lax.dynamic_index_in_dim(att_blocks, 1 - core, 2, keepdims=False)
    att_got = over_tensor(att_send, 1)
    att_a = att_mine.reshape(2, 2 * chunk, quarter)
    att_b = att_got.reshape(2, 2 * chunk, quarter)

    (
        out, grad_mid, gatt_a, gatt_b, inner_a, inner_b, normed_f,
        hid_a, hid_b, gh_a, gh_b, branch, gg_a, gg_f, gg_h,
    ) = middle(
        x_rows.reshape(2 * chunk, D), att_a, att_b, live, cot_rows.reshape(2 * chunk, D),
        proj_own, proj_other, up_own, up_other, down_own, down_other,
        gain_inner, ffn_gain.reshape(1, D), gain_hidden,
    )
    layer_out = swap_back(out.reshape(2, chunk, D))

    cot_own = cot_rows.reshape(2 * chunk, D)
    cot_got = over_tensor(cot_own, 1)
    hid_got = over_tensor(hid_b, 1)
    normf_got = over_tensor(normed_f, 1)
    gh_got = over_tensor(gh_b, 1)
    branch_got = over_tensor(branch, 1)
    inner_got = over_tensor(inner_b, 1)

    def two_sets(left, left_got, right, right_got):
        both = dot_tn(left, right) + dot_tn(left_got, right_got)
        return jnp.swapaxes(both.reshape(D, 2, -1), 0, 1)

    grad_down = scatter(two_sets(cot_own, cot_got, hid_a, hid_got))
    grad_up = scatter(two_sets(normed_f, normf_got, gh_a, gh_got))
    grad_proj = two_sets(branch, branch_got, inner_a, inner_got)

    gatt_got = over_tensor(gatt_b, 1)
    gatt = jnp.stack(
        [
            weave(gatt_a[k].reshape(2, chunk, quarter), gatt_got[k].reshape(2, chunk, quarter), core)
            for k in (0, 1)
        ]
    )
    grad_w, grad_n = attn_backward(normed, first_own, projected, lse_rows, gatt, doc_all)
    grad_first = scatter(jnp.concatenate([grad_w, grad_proj], axis=2))

    gn_blocks = grad_n.reshape(2, 2, chunk, D)
    gn_mine = lax.dynamic_index_in_dim(gn_blocks, core, 1, keepdims=False).reshape(2 * chunk, D)
    gn_send = lax.dynamic_index_in_dim(gn_blocks, 1 - core, 1, keepdims=False).reshape(2 * chunk, D)
    gn = gn_mine + over_tensor(gn_send.astype(BF), 1).astype(F4)
    gg_t = jnp.sum(gn * norm_t, axis=0)
    scaled = gn * attn_gain
    mean_s = jnp.mean(scaled, axis=-1, keepdims=True)
    mean_c = jnp.mean(scaled * norm_t, axis=-1, keepdims=True)
    grad_x = grad_mid + inv_t * (scaled - mean_s - norm_t * mean_c)
    grad_tokens = swap_back(grad_x.reshape(2, chunk, D))

    def place(vector, width):
        blocks = vector.reshape(4, width)
        order = [tensor_place, tensor_place ^ 2, tensor_place ^ 1, tensor_place ^ 3]
        full = jnp.zeros((4, width), F4)
        for k, where in enumerate(order):
            full = lax.dynamic_update_slice(full, blocks[k : k + 1], (where, 0))
        return full.reshape(1, -1)

    mid_gains = sum_everywhere(
        jnp.concatenate([gg_f, place(gg_a, quarter), place(gg_h, D)], axis=1)
    )
    total_ffn = mid_gains[0, :D]
    total_attn_inner = mid_gains[0, D : 2 * D].reshape(4, quarter)
    total_ffn_inner = mid_gains[0, 2 * D :].reshape(4, D)
    total_attn = sum_everywhere(gg_t.reshape(1, D))[0]
    return (
        layer_out,
        grad_tokens,
        total_attn,
        jnp.stack([grad_first[:, s * quarter : (s + 1) * quarter] for s in range(3)]),
        pick(total_attn_inner, tensor_place),
        grad_first[:, 3 * quarter :].T,
        total_ffn,
        grad_up,
        pick(total_ffn_inner, tensor_place),
        grad_down.T,
    )


def solution(mesh):
    in_specs = (
        P(None, ("dp", "tensor"), None),
        P(None, "dp"),
        P(None, "dp"),
        P(),
        P(None, "dp", "tensor"),
        P("tensor"),
        P("tensor", "dp"),
        P(),
        P("dp", "tensor"),
        P("tensor"),
        P("tensor", "dp"),
        P(None, ("dp", "tensor"), None),
    )
    out_specs = (
        P(None, ("dp", "tensor"), None),
        P(None, ("dp", "tensor"), None),
        P(),
        P(None, "dp", "tensor"),
        P("tensor"),
        P("tensor", "dp"),
        P(),
        P("dp", "tensor"),
        P("tensor"),
        P("tensor", "dp"),
    )
    return jax.shard_map(
        per_device, mesh=mesh, in_specs=in_specs, out_specs=out_specs, check_vma=False
    )
```

```python
import functools

import jax
import jax.numpy as jnp
from jax import lax
from jax.experimental import pallas as pl
from jax.experimental.pallas import tpu as pltpu
from jax.sharding import PartitionSpec as P

D = 768
HD = 64
FF = 3072
EPS = 1e-05
BLK = 256
PAIR = 1024
MIB = 1024 * 1024
VMEM = {'assemble': 12, 'second': 14, 'third': 9, 'tail': 9, 'attn_fwd': 20, 'attn_bwd': 30, 'grad_down': 26, 'grad_up': 36, 'middle': 42}
SCALE = HD ** (-0.5)
NEG = -1e30
BF = jnp.bfloat16
F4 = jnp.float32
SQRT_HALF = 0.7071067811865476
INV_SQRT_2PI = 0.3989422804014327


def dot_nn(a, b):
    return lax.dot_general(a, b, (((1,), (0,)), ((), ())), preferred_element_type=F4)


def dot_nt(a, b):
    return lax.dot_general(a, b, (((1,), (1,)), ((), ())), preferred_element_type=F4)


def dot_tn(a, b):
    return lax.dot_general(a, b, (((0,), (0,)), ((), ())), preferred_element_type=F4)


def over_tensor(value, bit):
    size = lax.axis_size("tensor")
    return lax.ppermute(value, "tensor", [(i, i ^ bit) for i in range(size)])


def over_dp_bit(value, bit):
    size = lax.axis_size("dp")
    return lax.ppermute(value, "dp", [(i, i ^ bit) for i in range(size)])


def over_z(value, step):
    size = lax.axis_size("dp")
    return lax.ppermute(value, "dp", [(i, (i + 2 * step) % size) for i in range(size)])


def after(value, *first):
    return lax.optimization_barrier((value,) + first)[0]


def gather_z(shard):
    one, two, three = (over_z(shard, k) for k in (1, 2, 3))
    return jnp.stack([shard, one]), jnp.stack([two, three])


def gather_xy_first(blocks):
    upper, lower = blocks
    return over_tensor(upper, 2), over_dp_bit(lower, 1)


def gather_xy_second(blocks, first):
    upper, lower = blocks
    upper_x, lower_y = first
    return (
        over_dp_bit(jnp.stack([upper, upper_x]), 1), over_tensor(jnp.stack([lower, lower_y]), 2)
    )


def assemble_kernel(place_ref, u_ref, l_ref, ux_ref, ly_ref, uy_ref, lx_ref, full_ref):
    z, y = place_ref[0], place_ref[1]
    rows = u_ref.shape[1]
    for k in range(4):
        for x_rel in range(2):
            for y_rel in range(2):
                if k < 2:
                    src = (ux_ref if x_rel else u_ref)[k] if y_rel == 0 else uy_ref[x_rel, k]
                else:
                    src = (
                        (ly_ref if y_rel else l_ref)[k - 2]
                        if x_rel == 0
                        else lx_ref[y_rel, k - 2]
                    )
                row = (lax.rem(z - k + 4, 4) * 2 + lax.rem(y + y_rel, 2)) * rows
                full_ref[x_rel, pl.ds(pl.multiple_of(row, 16), rows), :] = src


def assemble(blocks, first, second, place):
    cols = blocks[0].shape[-1]

    def all_of(a):
        return pl.BlockSpec(a.shape, lambda g, s: (0,) * a.ndim)

    return pl.pallas_call(
        assemble_kernel,
        grid_spec=pltpu.PrefetchScalarGridSpec(
            num_scalar_prefetch=1,
            grid=(1,),
            in_specs=[all_of(a) for a in (*blocks, *first, *second)],
            out_specs=pl.BlockSpec((2, D, cols), lambda g, s: (0, 0, 0)),
        ),
        out_shape=jax.ShapeDtypeStruct((2, D, cols), BF),
        cost_estimate=pl.CostEstimate(flops=0, transcendentals=0, bytes_accessed=8 * D * cols),
        compiler_params=pltpu.CompilerParams(vmem_limit_bytes=VMEM["assemble"] * MIB),
        name="assemble",
    )(place, *blocks, *first, *second)


def gather_any(shard):
    own = lax.all_gather(shard, "dp", axis=0, tiled=True)
    return jnp.stack([own, over_tensor(own, 2)])


def cut(place_ref, total_ref, x_rel, su_ref, sl_ref, ku_ref, kl_ref):
    z, y = place_ref[0], place_ref[1]
    rows = su_ref.shape[2]

    def block(j, y_rel):
        row = (lax.rem(z + j, 4) * 2 + lax.rem(y + y_rel, 2)) * rows
        return total_ref[pl.ds(pl.multiple_of(row, 8), rows), :]

    for j in range(2):
        su_ref[0, j] = block(j, 1).astype(BF)
        ku_ref[0, j] = block(j, 0)

    @pl.when(x_rel == 1)
    def _():
        for j in range(2):
            for y_rel in range(2):
                sl_ref[y_rel, j] = block(j + 2, y_rel).astype(BF)

    @pl.when(x_rel == 0)
    def _():
        for j in range(2):
            for y_rel in range(2):
                kl_ref[y_rel, j] = block(j + 2, y_rel)


def cut_specs(cols):
    shape = (2, 2, D // 8, cols)
    per = pl.BlockSpec((1,) + shape[1:], lambda g, s: (g, 0, 0, 0))
    whole = pl.BlockSpec(shape, lambda g, s: (0, 0, 0, 0))
    return [per, whole, per, whole], [jax.ShapeDtypeStruct(shape, t) for t in (BF, BF, F4, F4)]


def grad_kernel(place_ref, *refs, counts):
    total_ref = refs[-1]
    col, pos = 0, 0
    for count in counts:
        total = 0.0
        for left, right in zip(refs[pos : pos + count], refs[pos + count : pos + 2 * count]):
            part = right[0] if len(right.shape) == 3 else right[...]
            total = total + dot_tn(left[...], part)
        pos += 2 * count
        total_ref[:, col : col + total.shape[1]] = total
        col += total.shape[1]
    cut(place_ref, total_ref, pl.program_id(0), *refs[2 * sum(counts) : -1])


def width_of(right):
    return right.shape[-1] if right.ndim == 3 else right.shape[-1] // 2


def grad_parts(groups, place, name):
    cols = sum(width_of(rights[0]) for _, rights in groups)
    flat = [a for lefts, rights in groups for a in (*lefts, *rights)]

    def specs(lefts, rights):
        out = [pl.BlockSpec(a.shape, lambda g, s: (0, 0)) for a in lefts]
        for a in rights:
            if a.ndim == 3:
                out.append(pl.BlockSpec((1,) + a.shape[1:], lambda g, s: (g, 0, 0)))
            elif a.shape[1] % 256 == 0:
                out.append(pl.BlockSpec((a.shape[0], a.shape[1] // 2), lambda g, s: (0, g)))
        return out

    out_specs, out_shape = cut_specs(cols)
    return pl.pallas_call(
        functools.partial(grad_kernel, counts=tuple(len(lefts) for lefts, _ in groups)),
        grid_spec=pltpu.PrefetchScalarGridSpec(
            num_scalar_prefetch=1,
            grid=(2,),
            in_specs=[spec for group in groups for spec in specs(*group)],
            out_specs=out_specs,
            scratch_shapes=[pltpu.VMEM((D, cols), F4)],
        ),
        out_shape=out_shape,
        cost_estimate=pl.CostEstimate(
            flops=8 * D * cols * 512, transcendentals=0, bytes_accessed=24 * D * cols
        ),
        compiler_params=pltpu.CompilerParams(vmem_limit_bytes=VMEM[name] * MIB),
    )(place, *flat)


def grad_whole(groups):
    wide = []
    for lefts, rights in groups:
        total = 0.0
        for left, right in zip(lefts, rights):
            if right.ndim == 2:
                right = jnp.swapaxes(right.reshape(right.shape[0], 2, -1), 0, 1)
            total = total + jnp.einsum("td,xtc->xdc", left, right, preferred_element_type=F4)
        wide.append(total)
    return jnp.concatenate(wide, axis=2)


def second_kernel(*refs):
    su_ref, sl_ref, ku2_ref, kl2_ref = refs[-4:]
    at = 0
    for k in range(0, len(refs) - 4, 4):
        ku_ref, kl_ref, ru_ref, rl_ref = refs[k : k + 4]
        cols = slice(at, at + ku_ref.shape[-1])
        ku2_ref[:, :, cols] = ku_ref[0] + ru_ref[0].astype(F4)
        su_ref[:, :, cols] = (ku_ref[1] + ru_ref[1].astype(F4)).astype(BF)
        kl2_ref[:, :, cols] = kl_ref[0] + rl_ref[0].astype(F4)
        sl_ref[:, :, cols] = (kl_ref[1] + rl_ref[1].astype(F4)).astype(BF)
        at += ku_ref.shape[-1]


def third_kernel(ku_ref, kl_ref, ru_ref, rl_ref, s1_ref, s2_ref, s3_ref, keep_ref):
    keep_ref[...] = ku_ref[0] + ru_ref[0].astype(F4)
    s1_ref[...] = (ku_ref[1] + ru_ref[1].astype(F4)).astype(BF)
    s2_ref[...] = (kl_ref[0] + rl_ref[0].astype(F4)).astype(BF)
    s3_ref[...] = (kl_ref[1] + rl_ref[1].astype(F4)).astype(BF)


def add_call(kernel, shapes, args, name):
    return pl.pallas_call(
        kernel,
        out_shape=[jax.ShapeDtypeStruct(s, t) for s, t in shapes],
        cost_estimate=pl.CostEstimate(
            flops=0, transcendentals=0, bytes_accessed=3 * args[0].size * 4
        ),
        compiler_params=pltpu.CompilerParams(vmem_limit_bytes=VMEM[name[4:]] * MIB),
    )(*args)


def scatter_first(parts):
    return over_dp_bit(parts[0], 1), over_tensor(parts[1], 2)


def scatter_second(parts, got):
    shape = (2, D // 8, sum(p[0].shape[-1] for p in parts))
    args = [a for p, g in zip(parts, got) for a in (p[2], p[3], *g)]
    return add_call(
        second_kernel, [(shape, BF), (shape, BF), (shape, F4), (shape, F4)], args, "add_second"
    )


def scatter_second_send(parts):
    return over_tensor(parts[0], 2), over_dp_bit(parts[1], 1)


def scatter_third(parts, got):
    shape = parts[0].shape[1:]
    return add_call(
        third_kernel, [(shape, BF), (shape, BF), (shape, BF), (shape, F4)],
        (parts[2], parts[3]) + tuple(got), "add_third",
    )


def scatter_third_send(parts):
    return [over_z(parts[k], k + 1) for k in range(3)]


def scatter_end(parts, got):
    return parts[3] + got[0].astype(F4) + got[1].astype(F4) + got[2].astype(F4)


def scatter_any(grad):
    total = grad[0] + over_tensor(grad[1].astype(BF), 2).astype(F4)
    return lax.psum_scatter(total, "dp", scatter_dimension=0, tiled=True)


def attn_fwd_kernel(place_ref, *refs, first):
    core = place_ref[2]
    if first:
        (own_ref, got_ref, w_ref, doc_col_ref, doc_row_ref,
         proj_ref, mine_ref, send_ref, lse_ref, normed_ref, bias_ref, logs_ref, att_ref) = refs
    else:
        (normed_ref, bias_ref, w_ref,
         proj_ref, mine_ref, send_ref, lse_ref, logs_ref, att_ref) = refs
    rows = normed_ref.shape[0]
    blocks = rows // BLK
    if first:
        for i in range(blocks):
            there = pl.ds((i // 2) * BLK, BLK)
            normed_ref[pl.ds(i * BLK, BLK), :] = jnp.where(
                core == i % 2, own_ref[there, :], got_ref[there, :]
            )
            same = doc_col_ref[pl.ds(i * BLK, BLK), :] == doc_row_ref[:, : (i + 1) * BLK]
            row_id = i * BLK + lax.broadcasted_iota(jnp.int32, same.shape, 0)
            col_id = lax.broadcasted_iota(jnp.int32, same.shape, 1)
            bias_ref[pl.ds(i * BLK, BLK), : (i + 1) * BLK] = jnp.where(
                same & (col_id <= row_id), 0.0, NEG
            )
    proj_ref[...] = dot_nn(normed_ref[...], w_ref[0]).astype(BF)
    for h in range(3):
        keys = proj_ref[:, (3 + h) * HD : (4 + h) * HD]
        values = proj_ref[:, (6 + h) * HD : (7 + h) * HD]
        for i in range(blocks):
            span = (i + 1) * BLK
            here = pl.ds(i * BLK, BLK)
            query = proj_ref[here, h * HD : (h + 1) * HD] * BF(SCALE)
            scores = dot_nt(query, keys[:span]) + bias_ref[here, :span]
            peak = jnp.max(scores, axis=-1, keepdims=True)
            terms = jnp.exp(scores - peak)
            total = jnp.sum(terms, axis=-1, keepdims=True)
            mixed = dot_nn(terms.astype(BF), values[:span]) / total
            att_ref[here, h * HD : (h + 1) * HD] = mixed
            logs_ref[here, h : h + 1] = peak + jnp.log(total)
    lse_ref[...] = logs_ref[...].T[:8]
    for j in range(blocks // 2):
        here = pl.ds(j * BLK, BLK)
        even = att_ref[pl.ds(2 * j * BLK, BLK), :]
        odd = att_ref[pl.ds((2 * j + 1) * BLK, BLK), :]
        mine_ref[here, : 3 * HD] = jnp.where(core == 0, even, odd)
        send_ref[here, : 3 * HD] = jnp.where(core == 0, odd, even)


def attn_forward(place, weights, x_rel, *, tokens=None, again=None):
    first = tokens is not None
    half = (tokens[0].shape[0]) if first else again[0].shape[0] // 2
    rows = 2 * half
    whole = lambda g, s: (0, 0)
    w_spec = pl.BlockSpec((1, D, 9 * HD), lambda g, s: (x_rel, 0, 0))

    def all_of(shape):
        return pl.BlockSpec(shape, whole)

    shapes = [
        ((rows, 9 * HD), BF), ((half, 4 * HD), F4), ((half, 4 * HD), F4), ((8, rows), F4),
    ]
    if first:
        own, got, doc_col, doc_row = tokens
        shapes += [((rows, D), BF), ((rows, rows), F4)]
        args = (own, got, weights, doc_col, doc_row)
        in_specs = [
            all_of((half, D)), all_of((half, D)), w_spec, all_of((rows, 1)), all_of((1, rows)),
        ]
    else:
        args = (*again, weights)
        in_specs = [all_of((rows, D)), all_of((rows, rows)), w_spec]
    return pl.pallas_call(
        functools.partial(attn_fwd_kernel, first=first),
        grid_spec=pltpu.PrefetchScalarGridSpec(
            num_scalar_prefetch=1,
            grid=(1,),
            in_specs=in_specs,
            out_specs=[all_of(shape) for shape, _ in shapes],
            scratch_shapes=[pltpu.VMEM((rows, 128), F4), pltpu.VMEM((rows, 3 * HD), F4)],
        ),
        out_shape=[jax.ShapeDtypeStruct(*st) for st in shapes],
        cost_estimate=pl.CostEstimate(
            flops=rows * D * 18 * HD + 2 * 6 * rows * rows * HD,
            transcendentals=6 * rows * rows // 4,
            bytes_accessed=8 * rows * D,
        ),
        compiler_params=pltpu.CompilerParams(vmem_limit_bytes=VMEM["attn_fwd"] * MIB),
    )(place, *args)


def attn_bwd_kernel(
    place_ref, w_ref, proj_a_ref, proj_b_ref, lse_a_ref, lse_b_ref, own_ref, got_ref,
    doc_col_ref, doc_row_ref, normed_ref, *refs, ring,
):
    if ring:
        parts, refs = refs[:4], refs[4:]
        mine_ref, send_ref, gp_ref, gw_ref = *refs[:2], *refs[-2:]
        bias_ref, gk_ref, gv_ref, ga_ref, dn_ref, proj_ref, lse_ref = refs[2:-2]
    else:
        gp_ref, mine_ref, send_ref = refs[:3]
        bias_ref, gk_ref, gv_ref, ga_ref, dn_ref, proj_ref, lse_ref = refs[3:]
    core = place_ref[2]
    rows = dn_ref.shape[0]
    blocks = rows // BLK

    @pl.when(pl.program_id(0) == 0)
    def _():
        for i in range(blocks):
            span = (i + 1) * BLK
            same = doc_col_ref[:span, :] == doc_row_ref[:, i * BLK : span]
            key_id = lax.broadcasted_iota(jnp.int32, same.shape, 0)
            query_id = i * BLK + lax.broadcasted_iota(jnp.int32, same.shape, 1)
            bias_ref[:span, i * BLK : span] = jnp.where(same & (key_id <= query_id), 0.0, NEG)

    for x_rel, p_ref, l_ref in ((0, proj_a_ref, lse_a_ref), (1, proj_b_ref, lse_b_ref)):

        @pl.when(pl.program_id(0) == x_rel)
        def _(x_rel=x_rel, p_ref=p_ref, l_ref=l_ref):
            proj_ref[0] = p_ref[...]
            lse_ref[0] = l_ref[...]
            cols = slice(x_rel * 3 * HD, (x_rel + 1) * 3 * HD)
            for i in range(blocks):
                there = pl.ds((i // 2) * BLK, BLK)
                ga_ref[pl.ds(i * BLK, BLK), :] = jnp.where(
                    core == i % 2, own_ref[there, cols], got_ref[there, cols]
                )

    for h in range(3):
        keys = proj_ref[0, :, (3 + h) * HD : (4 + h) * HD]
        values = proj_ref[0, :, (6 + h) * HD : (7 + h) * HD]
        for i in reversed(range(blocks)):
            span = (i + 1) * BLK
            here = pl.ds(i * BLK, BLK)
            query = proj_ref[0, here, h * HD : (h + 1) * HD] * BF(SCALE)
            grad_rows = ga_ref[here, h * HD : (h + 1) * HD]
            scores = dot_nt(keys[:span], query) + bias_ref[:span, here]
            probs = jnp.exp(scores - lse_ref[0, h : h + 1, here])
            grad_probs = dot_nt(values[:span], grad_rows)
            inner = jnp.sum(probs * grad_probs, axis=0, keepdims=True)
            grad_scores = (probs * (grad_probs - inner)).astype(BF)
            add_v = dot_nn(probs.astype(BF), grad_rows)
            add_k = dot_nn(grad_scores, query)
            if span == rows:
                gv_ref[...] = add_v
                gk_ref[...] = add_k
            else:
                gv_ref[:span] += add_v
                gk_ref[:span] += add_k
            gp_ref[0, here, h * HD : (h + 1) * HD] = (
                dot_tn(grad_scores, keys[:span]) * SCALE
            ).astype(BF)
        gp_ref[0, :, (3 + h) * HD : (4 + h) * HD] = gk_ref[...].astype(BF)
        gp_ref[0, :, (6 + h) * HD : (7 + h) * HD] = gv_ref[...].astype(BF)
    back = dot_nt(gp_ref[0], w_ref[0])
    if ring:
        gw_ref[...] = dot_tn(normed_ref[...], gp_ref[0])
        cut(place_ref, gw_ref, pl.program_id(0), *parts)

    @pl.when(pl.program_id(0) == 0)
    def _():
        dn_ref[...] = back

    @pl.when(pl.program_id(0) == 1)
    def _():
        for i in range(blocks):
            there = pl.ds((i // 2) * BLK, BLK)
            here = pl.ds(i * BLK, BLK)

            @pl.when(core == i % 2)
            def _(there=there, here=here, i=i):
                mine_ref[there, :] = dn_ref[here, :] + back[i * BLK : (i + 1) * BLK]

            @pl.when(core != i % 2)
            def _(there=there, here=here, i=i):
                send_ref[there, :] = (dn_ref[here, :] + back[i * BLK : (i + 1) * BLK]).astype(BF)


def attn_backward(place, weights, projected, lse, own, got, doc_col, doc_row, normed, ring):
    half = own.shape[0]
    rows = 2 * half
    whole = lambda g, s: (0, 0)
    per = lambda g, s: (g, 0, 0)
    if ring:
        first_specs, first_shapes = cut_specs(9 * HD)
        more = [pltpu.VMEM((1, rows, 9 * HD), BF), pltpu.VMEM((D, 9 * HD), F4)]
    else:
        first_specs = [pl.BlockSpec((1, rows, 9 * HD), per)]
        first_shapes = [jax.ShapeDtypeStruct((2, rows, 9 * HD), BF)]
        more = []
    return pl.pallas_call(
        functools.partial(attn_bwd_kernel, ring=ring),
        grid_spec=pltpu.PrefetchScalarGridSpec(
            num_scalar_prefetch=1,
            grid=(2,),
            in_specs=[
                pl.BlockSpec((1, D, 9 * HD), per),
                pl.BlockSpec((rows, 9 * HD), whole),
                pl.BlockSpec((rows, 9 * HD), whole),
                pl.BlockSpec((8, rows), whole),
                pl.BlockSpec((8, rows), whole),
                pl.BlockSpec((half, 6 * HD), whole),
                pl.BlockSpec((half, 6 * HD), whole),
                pl.BlockSpec((rows, 1), whole),
                pl.BlockSpec((1, rows), whole),
                pl.BlockSpec((rows, D), whole),
            ],
            out_specs=first_specs + [pl.BlockSpec((half, D), whole)] * 2,
            scratch_shapes=[
                pltpu.VMEM((rows, rows), F4),
                pltpu.VMEM((rows, HD), F4),
                pltpu.VMEM((rows, HD), F4),
                pltpu.VMEM((rows, 3 * HD), BF),
                pltpu.VMEM((rows, D), F4),
                pltpu.VMEM((1, rows, 9 * HD), BF),
                pltpu.VMEM((1, 8, rows), F4),
                *more,
            ],
        ),
        out_shape=first_shapes
        + [jax.ShapeDtypeStruct((half, D), F4), jax.ShapeDtypeStruct((half, D), BF)],
        cost_estimate=pl.CostEstimate(
            flops=2 * rows * D * 18 * HD + 10 * 6 * rows * rows * HD,
            transcendentals=6 * rows * rows // 2,
            bytes_accessed=16 * rows * D,
        ),
        compiler_params=pltpu.CompilerParams(vmem_limit_bytes=VMEM["attn_bwd"] * MIB),
        name="attn_bwd",
    )(place, weights, *projected, *lse, own, got, doc_col, doc_row, normed)


def row_stats(values, width):
    mean = jnp.sum(values, axis=-1, keepdims=True) / width
    var = jnp.sum(values * values, axis=-1, keepdims=True) / width - mean * mean
    return mean, lax.rsqrt(var + EPS)


def middle_kernel(
    place_ref, xin_ref, att_0_ref, att_1_ref, att_2_ref, att_3_ref, live_ref, cot_ref,
    up_a_ref, up_b_ref, down_a_ref, down_b_ref,
    gain_a_ref, gain_f_ref, gain_h_ref,
    keep_ref, send_ref, gmid_ref, gatt_a_ref, gatt_b_ref, inner_a_ref, inner_b_ref, normf_ref,
    hid_a_ref, hid_b_ref, gh_a_ref, gh_b_ref, branch_ref, gg_a_ref, gg_f_ref, gg_h_ref,
    act_ref, slope_ref, scaled_ref,
):
    first = pl.program_id(0) == 0
    live = live_ref[...]
    att = jnp.concatenate(
        [ref[:, : 3 * HD] for ref in (att_0_ref, att_1_ref, att_2_ref, att_3_ref)], axis=1
    ) * live
    mean_a, inv_a = row_stats(att, D)
    norm_a = (att - mean_a) * inv_a
    gain_a = gain_a_ref[...]
    inner = (norm_a * gain_a).astype(BF)
    quarter = 3 * HD
    for k, ref in ((0, inner_a_ref), (2, inner_b_ref)):
        ref[:, :quarter] = inner[:, k * quarter : (k + 1) * quarter]
        ref[:, 256 : 256 + quarter] = inner[:, (k + 1) * quarter : (k + 2) * quarter]
        ref[:, quarter:256] = jnp.zeros((BLK, 256 - quarter), BF)
        ref[:, 256 + quarter :] = jnp.zeros((BLK, 256 - quarter), BF)
    proj_t = jnp.concatenate(
        [ref[k, :, D : D + 3 * HD] for ref in (up_a_ref, up_b_ref) for k in (0, 1)], axis=1
    )
    mid = xin_ref[...].astype(F4) + dot_nt(inner, proj_t)
    mean_f, inv_f = row_stats(mid, D)
    norm_f = (mid - mean_f) * inv_f
    gain_f = gain_f_ref[...]
    normed_f = (norm_f * gain_f).astype(BF)
    normf_ref[...] = normed_f

    ups = [(up_a_ref, 0), (up_a_ref, 1), (up_b_ref, 0), (up_b_ref, 1)]
    downs = [(down_a_ref, 0), (down_a_ref, 1), (down_b_ref, 0), (down_b_ref, 1)]
    total = 0.0
    square = 0.0
    for j, (ref, k) in enumerate(ups):
        hidden = dot_nn(normed_f, ref[k, :, :D])
        phi = 0.5 * (1.0 + lax.erf(hidden * SQRT_HALF))
        act = hidden * phi
        slope_ref[j] = phi + hidden * (INV_SQRT_2PI * jnp.exp(-0.5 * hidden * hidden))
        act_ref[j] = act
        total += jnp.sum(act, axis=-1, keepdims=True)
        square += jnp.sum(act * act, axis=-1, keepdims=True)
    mean_h = total / FF
    inv_h = lax.rsqrt(square / FF - mean_h * mean_h + EPS)
    cot = cot_ref[...]
    out = mid
    sum_s = 0.0
    sum_c = 0.0
    for j, (ref, k) in enumerate(downs):
        norm_h = (act_ref[j] - mean_h) * inv_h
        act_ref[j] = norm_h
        gain_h = gain_h_ref[:, j * D : (j + 1) * D]
        low = (norm_h * gain_h).astype(BF)
        if j < 2:
            hid_a_ref[:, j * D : (j + 1) * D] = low
        else:
            hid_b_ref[:, (j - 2) * D : (j - 1) * D] = low
        out = out + dot_nt(low, ref[k])
        grad_low = dot_nn(cot, ref[k])
        crossed = grad_low * norm_h
        gain_part = jnp.sum(crossed, axis=0, keepdims=True)

        @pl.when(first)
        def _(gain_part=gain_part, j=j):
            gg_h_ref[:, j * D : (j + 1) * D] = gain_part

        @pl.when(jnp.logical_not(first))
        def _(gain_part=gain_part, j=j):
            gg_h_ref[:, j * D : (j + 1) * D] += gain_part

        scaled = grad_low * gain_h
        scaled_ref[j] = scaled
        sum_s += jnp.sum(scaled, axis=-1, keepdims=True)
        sum_c += jnp.sum(crossed * gain_h, axis=-1, keepdims=True)

    @pl.when(pl.program_id(0) == place_ref[3])
    def _():
        keep_ref[...] = out

    @pl.when(pl.program_id(0) != place_ref[3])
    def _():
        send_ref[...] = out.astype(BF)

    mean_s = sum_s / FF
    mean_c = sum_c / FF
    grad_n = 0.0
    for j, (ref, k) in enumerate(ups):
        grad_act = inv_h * (scaled_ref[j] - mean_s - act_ref[j] * mean_c)
        grad_hidden = (grad_act * slope_ref[j]).astype(BF)
        if j < 2:
            gh_a_ref[:, j * D : (j + 1) * D] = grad_hidden
        else:
            gh_b_ref[:, (j - 2) * D : (j - 1) * D] = grad_hidden
        grad_n = grad_n + dot_nt(grad_hidden, ref[k, :, :D])
    gain_part_f = jnp.sum(grad_n * norm_f, axis=0, keepdims=True)
    scaled = grad_n * gain_f
    mean_s = jnp.sum(scaled, axis=-1, keepdims=True) / D
    mean_c = jnp.sum(scaled * norm_f, axis=-1, keepdims=True) / D
    grad_mid = cot.astype(F4) + inv_f * (scaled - mean_s - norm_f * mean_c)
    gmid_ref[...] = grad_mid
    branch = grad_mid.astype(BF)
    branch_ref[...] = branch
    grad_inner = dot_nn(branch, proj_t)
    gain_part_a = jnp.sum(grad_inner * norm_a, axis=0, keepdims=True)
    scaled = grad_inner * gain_a
    mean_s = jnp.sum(scaled, axis=-1, keepdims=True) / D
    mean_c = jnp.sum(scaled * norm_a, axis=-1, keepdims=True) / D
    grad_att = (inv_a * (scaled - mean_s - norm_a * mean_c) * live).astype(BF)
    gatt_a_ref[...] = grad_att[:, : D // 2]
    gatt_b_ref[...] = grad_att[:, D // 2 :]

    @pl.when(first)
    def _():
        gg_f_ref[...] = gain_part_f
        gg_a_ref[...] = gain_part_a

    @pl.when(jnp.logical_not(first))
    def _():
        gg_f_ref[...] += gain_part_f
        gg_a_ref[...] += gain_part_a


def middle(place, xin, att, live, cot, up_a, up_b, down_a, down_b, gain_a, gain_f, gain_h):
    rows = xin.shape[0]
    once = pl.Buffered(1)
    fixed = lambda g, s: (0, 0)

    def rows_of(width):
        return pl.BlockSpec((BLK, width), lambda g, s: (g, 0))

    def whole(width):
        return pl.BlockSpec((2, D, width), lambda g, s: (0, 0, 0), pipeline_mode=once)

    def vec(width):
        return pl.BlockSpec((1, width), fixed)

    outs = [
        (pl.BlockSpec((BLK, D), fixed), (BLK, D), F4),
        (pl.BlockSpec((BLK, D), fixed), (BLK, D), BF),
        (rows_of(D), (rows, D), F4),
        (rows_of(D // 2), (rows, D // 2), BF),
        (rows_of(D // 2), (rows, D // 2), BF),
        (rows_of(512), (rows, 512), BF),
        (rows_of(512), (rows, 512), BF),
        (rows_of(D), (rows, D), BF),
        (rows_of(FF // 2), (rows, FF // 2), BF),
        (rows_of(FF // 2), (rows, FF // 2), BF),
        (rows_of(FF // 2), (rows, FF // 2), BF),
        (rows_of(FF // 2), (rows, FF // 2), BF),
        (rows_of(D), (rows, D), BF),
        (vec(D), (1, D), F4),
        (vec(D), (1, D), F4),
        (vec(FF), (1, FF), F4),
    ]
    return pl.pallas_call(
        middle_kernel,
        grid_spec=pltpu.PrefetchScalarGridSpec(
            num_scalar_prefetch=1,
            grid=(rows // BLK,),
            in_specs=[
                rows_of(D), *[rows_of(4 * HD)] * 4, rows_of(1), rows_of(D),
                whole(PAIR), whole(PAIR), whole(D), whole(D),
                vec(D), vec(D), vec(FF),
            ],
            out_specs=[o[0] for o in outs],
            scratch_shapes=[pltpu.VMEM((4, BLK, D), F4)] * 3,
        ),
        out_shape=[jax.ShapeDtypeStruct(o[1], o[2]) for o in outs],
        cost_estimate=pl.CostEstimate(
            flops=4 * rows * D * (D + 2 * FF),
            transcendentals=2 * rows * FF,
            bytes_accessed=22 * 1024 * 1024,
        ),
        compiler_params=pltpu.CompilerParams(vmem_limit_bytes=VMEM["middle"] * MIB),
        name="middle",
    )(place, xin, *att, live, cot, up_a, up_b, down_a, down_b, gain_a, gain_f, gain_h)


def tail_kernel(place_ref, x_ref, mine_ref, got_ref, gmid_ref, gain_ref, keep_ref, send_ref, gg_ref):
    xin = x_ref[...].astype(F4)
    mean, inv = row_stats(xin, D)
    norm = (xin - mean) * inv
    grad = mine_ref[...] + got_ref[...].astype(F4)
    scaled = grad * gain_ref[...]
    mean_s = jnp.sum(scaled, axis=-1, keepdims=True) / D
    mean_c = jnp.sum(scaled * norm, axis=-1, keepdims=True) / D
    full = gmid_ref[...] + inv * (scaled - mean_s - norm * mean_c)
    gain_part = jnp.sum(grad * norm, axis=0, keepdims=True)

    @pl.when(pl.program_id(0) == 0)
    def _():
        send_ref[...] = full.astype(BF)
        gg_ref[...] = gain_part

    @pl.when(pl.program_id(0) == 1)
    def _():
        keep_ref[...] = full
        gg_ref[...] += gain_part


def tail(place, x_rows, mine, got, gmid, gain):
    block = pl.BlockSpec((BLK, D), lambda g, s: ((g + 1 + s[3]) % 2, 0))
    fixed = lambda g, s: (0, 0)
    return pl.pallas_call(
        tail_kernel,
        grid_spec=pltpu.PrefetchScalarGridSpec(
            num_scalar_prefetch=1,
            grid=(2,),
            in_specs=[block, block, block, block, pl.BlockSpec((1, D), fixed)],
            out_specs=[
                pl.BlockSpec((BLK, D), fixed),
                pl.BlockSpec((BLK, D), fixed),
                pl.BlockSpec((1, D), fixed),
            ],
        ),
        out_shape=[
            jax.ShapeDtypeStruct((BLK, D), F4),
            jax.ShapeDtypeStruct((BLK, D), BF),
            jax.ShapeDtypeStruct((1, D), F4),
        ],
        cost_estimate=pl.CostEstimate(flops=0, transcendentals=0, bytes_accessed=12 * BLK * D),
        compiler_params=pltpu.CompilerParams(vmem_limit_bytes=VMEM["tail"] * MIB),
        name="tail",
    )(place, x_rows, mine, got, gmid, gain)


def per_device(
    tokens,
    doc_ids,
    live_mask,
    attn_gain,
    qkv_weight,
    attn_inner_gain,
    proj_weight,
    ffn_gain,
    up_weight,
    ffn_inner_gain,
    down_weight,
    cotangent,
):
    ring = lax.axis_size("dp") == 8
    tensor_place = lax.axis_index("tensor")
    dp_place = lax.axis_index("dp")
    side = tensor_place // 2
    core = tensor_place % 2
    place = jnp.stack([dp_place // 2, dp_place % 2, core, side]).astype(jnp.int32)
    chunk = tokens.shape[1]
    quarter = 3 * HD

    def pick(pair, index):
        return lax.dynamic_index_in_dim(pair, index, 0, keepdims=False)

    def in_order(own, other):
        return jnp.where(side == 0, jnp.stack([own, other]), jnp.stack([other, own]))

    shard_1 = jnp.concatenate([qkv_weight[0], qkv_weight[1], qkv_weight[2]], axis=1)
    shard_2 = jnp.concatenate(
        [up_weight, proj_weight.T, jnp.zeros((up_weight.shape[0], PAIR - D - quarter), BF)], axis=1
    )
    shard_3 = down_weight.T
    token_other = over_tensor(pick(tokens, 1 - side), 2)
    cot_other = over_tensor(pick(cotangent, 1 - side), 2)
    if ring:
        blocks_1 = gather_z(shard_1)
        first_1 = gather_xy_first(blocks_1)
        shard_2 = after(shard_2, *blocks_1)
        blocks_2 = gather_z(shard_2)
        second_1 = gather_xy_second(blocks_1, first_1)
        w_1 = assemble(blocks_1, first_1, second_1, place)
        first_2 = gather_xy_first(blocks_2)
        blocks_3 = gather_z(after(shard_3, *blocks_2))
        second_2 = gather_xy_second(blocks_2, first_2)
        w_2 = assemble(blocks_2, first_2, second_2, place)
        first_3 = gather_xy_first(blocks_3)
        second_3 = gather_xy_second(blocks_3, first_3)
        w_3 = assemble(blocks_3, first_3, second_3, place)
    else:
        w_1, w_2, w_3 = (gather_any(s) for s in (shard_1, shard_2, shard_3))
    w_2_other = over_tensor(w_2, 1)
    w_3_other = over_tensor(w_3, 1)

    gains = jnp.concatenate([attn_inner_gain, ffn_inner_gain]).reshape(1, -1)
    gain_pair = jnp.concatenate([gains, over_tensor(gains, 1)])
    gain_far = over_tensor(gain_pair, 2)
    gain_all = jnp.stack([gain_pair[0], gain_far[0], gain_pair[1], gain_far[1]])
    gain_inner = gain_all[:, :quarter].reshape(1, D)
    gain_hidden = gain_all[:, quarter:].reshape(1, FF)

    x_rows = in_order(pick(tokens, side), token_other).reshape(2 * chunk, D)
    cot_rows = in_order(pick(cotangent, side), cot_other).reshape(2 * chunk, D)
    doc_all = pick(doc_ids, side)
    doc_col, doc_row = doc_all.reshape(-1, 1), doc_all.reshape(1, -1)
    live_all = pick(live_mask, side).astype(F4).reshape(2, 2, chunk)
    live = lax.dynamic_index_in_dim(live_all, core, 1, keepdims=False).reshape(2 * chunk, 1)
    xin = x_rows.astype(F4)
    mean_t, inv_t = row_stats(xin, D)
    normed_own = ((xin - mean_t) * inv_t * attn_gain).astype(BF)
    attn_gain_row, ffn_gain_row = attn_gain.reshape(1, D), ffn_gain.reshape(1, D)
    normed_own, doc_col, doc_row, live, attn_gain_row, ffn_gain_row = lax.optimization_barrier(
        (normed_own, doc_col, doc_row, live, attn_gain_row, ffn_gain_row)
    )
    normed_got = over_tensor(normed_own, 1)

    proj_0, mine_0, send_0, lse_0, normed, bias = attn_forward(
        place, w_1, 0, tokens=(normed_own, normed_got, doc_col, doc_row)
    )
    proj_1, mine_1, send_1, lse_1 = attn_forward(place, w_1, 1, again=(normed, bias))
    att = (mine_0, mine_1, over_tensor(send_0, 1), over_tensor(send_1, 1))
    (
        out_keep, out_send, grad_mid, gatt_own, gatt_send, inner_a, inner_b, normed_f,
        hid_a, hid_b, gh_a, gh_b, branch, gg_a, gg_f, gg_h,
    ) = middle(
        place, x_rows, att, live, cot_rows, w_2, w_2_other, w_3, w_3_other,
        gain_inner, ffn_gain_row, gain_hidden,
    )
    gatt_got = over_tensor(gatt_send, 1)
    out_got = over_tensor(out_send, 2)
    layer_out = in_order(out_keep, out_got.astype(F4))

    group_3 = [((cot_rows, over_tensor(cot_rows, 1)), (hid_a, over_tensor(hid_b, 1)))]
    group_2 = [
        ((normed_f, over_tensor(normed_f, 1)), (gh_a, over_tensor(gh_b, 1))),
        ((branch, over_tensor(branch, 1)), (inner_a, over_tensor(inner_b, 1))),
    ]
    if ring:
        parts_3 = grad_parts(group_3, place, "grad_down")
        got_3 = scatter_first(parts_3)
        parts_2 = grad_parts(group_2, place, "grad_up")
        got_2 = scatter_first(parts_2)
    *parts_1, dn_mine, dn_send = attn_backward(
        place, w_1, (proj_0, proj_1), (lse_0, lse_1), gatt_own, gatt_got, doc_col, doc_row,
        normed, ring,
    )
    dn_got = over_tensor(dn_send, 1)
    if ring:
        got_1 = scatter_first(parts_1)
        parts_2 = scatter_second((parts_3, parts_2), (got_3, got_2))
        got_2 = scatter_second_send(parts_2)
        parts_1 = scatter_second((parts_1,), (got_1,))
        got_1 = scatter_second_send(parts_1)
        parts_2 = scatter_third(parts_2, got_2)
        got_2 = scatter_third_send(parts_2)
        parts_1 = scatter_third(parts_1, got_1)
        got_1 = scatter_third_send(parts_1)
        total_1 = scatter_end(parts_1, got_1)
        total_2 = scatter_end(parts_2, got_2)
        total_3, total_2 = total_2[:, :D], total_2[:, D:]
    else:
        total_3, total_2, total_1 = (
            scatter_any(grad_whole(g)) for g in (group_3, group_2, [((normed,), parts_1)])
        )

    tok_keep, tok_send, gg_t = tail(place, x_rows, dn_mine, dn_got, grad_mid, attn_gain_row)
    grad_tokens = in_order(tok_keep, over_tensor(tok_send, 2).astype(F4))

    split = jnp.concatenate([gg_a.reshape(4, quarter), gg_h.reshape(4, D)], axis=1)
    whole = jnp.concatenate([gg_f, gg_t], axis=1)
    vector = jnp.concatenate([whole, split.reshape(1, -1)], axis=1)
    step = over_tensor(vector, 1)
    whole = whole + step[:, : 2 * D]
    split = split[:2] + step[:, 2 * D :].reshape(4, -1)[2:]
    vector = jnp.concatenate([whole, split.reshape(1, -1)], axis=1)
    bit = lax.axis_size("dp") // 2
    while bit > 1:
        vector = vector + over_dp_bit(vector, bit)
        bit //= 2
    step = over_tensor(vector, 2)
    whole = vector[:, : 2 * D] + step[:, : 2 * D]
    split = vector[:, 2 * D :].reshape(2, -1)[:1] + step[:, 2 * D :].reshape(2, -1)[1:]
    vector = jnp.concatenate([whole, split], axis=1)
    vector = vector + over_dp_bit(vector, 1)
    vector = vector[0]
    return (
        layer_out,
        grad_tokens,
        vector[D : 2 * D],
        jnp.stack([total_1[:, s * quarter : (s + 1) * quarter] for s in range(3)]),
        vector[2 * D : 2 * D + quarter],
        total_2[:, D : D + quarter].T,
        vector[:D],
        total_2[:, :D],
        vector[2 * D + quarter :],
        total_3.T,
    )


def solution(mesh):
    in_specs = (
        P(None, ("dp", "tensor"), None),
        P(None, "dp"),
        P(None, "dp"),
        P(),
        P(None, "dp", "tensor"),
        P("tensor"),
        P("tensor", "dp"),
        P(),
        P("dp", "tensor"),
        P("tensor"),
        P("tensor", "dp"),
        P(None, ("dp", "tensor"), None),
    )
    out_specs = (
        P(None, ("dp", "tensor"), None),
        P(None, ("dp", "tensor"), None),
        P(),
        P(None, "dp", "tensor"),
        P("tensor"),
        P("tensor", "dp"),
        P(),
        P("dp", "tensor"),
        P("tensor"),
        P("tensor", "dp"),
    )

    return jax.shard_map(
        per_device, mesh=mesh, in_specs=in_specs, out_specs=out_specs, check_vma=False
    )
```
